32 devices in a mesh: dp: 8 (over z, y), tensor: 4 (over x, core).
Axes of the slice: x: 2, y: 2, z: 4, core: 2. Of those that a mesh axis runs over, the one named last changes fastest.
Arguments:
- gradients: bfloat16 [8, 2, 256, 1792], P('dp', None, None, 'tensor'), may hold values from -16 to 16, as said below
- errors: float32 [8, 2, 256, 1792], P('dp', None, None, 'tensor'), may hold values from -4 to 4
- start_factors: float32 [2, 1792, 32], P(None, 'tensor'), may hold values from -5 to 5
- moments: float32 [2, 256, 1792], P(None, 'dp', 'tensor'), may hold values from -2 to 2
- weights: float32 [2, 256, 1792], P(None, 'dp', 'tensor'), may hold values from -5 to 5
- vector_grads: bfloat16 [8, 5, 1792], P('dp', None, 'tensor'), may hold values from -16 to 16, as said below
- vector_moments: float32 [5, 1792], P(None, 'tensor'), may hold values from -2 to 2
- vector_weights: float32 [5, 1792], P(None, 'tensor'), may hold values from 0.5 to 1.5
Outputs:
- new_errors: float32 [8, 2, 256, 1792], P('dp', None, None, 'tensor')
- new_moments: float32 [2, 256, 1792], P(None, 'dp', 'tensor')
- new_weights: bfloat16 [2, 256, 1792], P(None, None, 'tensor')
- new_vector_moments: float32 [5, 1792], P(None, 'tensor')
- new_vector_weights: float32 [5, 1792], P(None, 'tensor')
The draws below stay inside these ranges and needn't reach their ends.
Inputs may be any that keep to these rules, and one draw needn't show every extreme that they name: `gradients`: each replica's gradient is a part common to all replicas plus its own part. `vector_grads`: each replica's gradient is a part common to all replicas plus its own part.
All inputs are finite; a program needn't handle non-finite values.
Results may differ from the reference program's by a relative error of at most 0.0004.
Values may be sent and summed in bfloat16 or wider, within the bound.
A program may use at most 64 MiB of HBM per device.

```python
import jax
import jax.numpy as jnp
from jax import lax

D = 1792
QK = 256
RANK = 32
ROUNDS = 2
MATS = 2
VROWS = 5
REPLICAS = 8


def replica_law(key, inner):
    first, second = jax.random.split(key, 2)
    replica_idx = jnp.arange(REPLICAS, dtype=jnp.float32)
    spread = 1.0 + 2.0 * replica_idx / max(REPLICAS - 1, 1)
    spread = spread.reshape((REPLICAS,) + (1,) * len(inner))
    common = jnp.clip(jax.random.normal(first, inner, jnp.float32), -4.0, 4.0)
    own_part = jnp.clip(jax.random.normal(second, (REPLICAS,) + inner, jnp.float32), -4.0, 4.0)
    return common[None] + own_part * spread


def draw_gradients(key, part):
    return replica_law(jax.random.fold_in(key, 11), (MATS, QK, D)).astype(jnp.bfloat16)


def draw_vector_grads(key, part):
    return replica_law(jax.random.fold_in(key, 23), (VROWS, D)).astype(jnp.bfloat16)


def block_levels(rng, dims, pieces, smallest, high):
    loudness = 1.0
    for axis_at, blocks in pieces:
        draws = jax.random.uniform(jax.random.fold_in(jax.random.fold_in(rng, 6), axis_at), (blocks,), jnp.float32, smallest / len(pieces), high / len(pieces))
        loudness = loudness * jnp.repeat(jnp.exp(draws), dims[axis_at] // blocks).reshape((-1,) + (1,) * (len(dims) - 1 - axis_at))
    return loudness


def normal_values(key, extent, scale, reach, cuts=(), kind=jnp.bfloat16):
    level = block_levels(key, extent, cuts, -0.22, 0.18) if cuts else 1.0
    entries = jax.random.normal(key, extent, jnp.float32) * scale * level
    return jnp.minimum(jnp.maximum(entries, -reach), reach).astype(kind)


def setup_inputs(seed: int = 0) -> dict:
    splits = jax.random.split(jax.random.key(seed), 9)
    return {
        "gradients": draw_gradients(jax.random.fold_in(splits[8], 71), 0),
        "errors": normal_values(splits[1], (REPLICAS, MATS, QK, D), 0.5, 4.0, ((0, 8), (3, 4)), jnp.float32),
        "start_factors": normal_values(splits[2], (MATS, D, RANK), 1.0, 5.0, ((1, 4),), jnp.float32),
        "moments": normal_values(splits[3], (MATS, QK, D), 0.3, 2.0, ((1, 8), (2, 4)), jnp.float32),
        "weights": normal_values(splits[4], (MATS, QK, D), 1.0, 5.0, ((1, 8), (2, 4)), jnp.float32),
        "vector_grads": draw_vector_grads(jax.random.fold_in(splits[8], 71), 0),
        "vector_moments": normal_values(splits[6], (VROWS, D), 0.3, 2.0, ((1, 4),), jnp.float32),
        "vector_weights": jnp.clip(1.0 + 0.1 * jax.random.normal(splits[7], (VROWS, D), jnp.float32), 0.5, 1.5),
    }


momentum_coef = 0.9
step_rate = 0.1

def orthonormal(summed):
    gram_mat = jnp.dot(summed.T, summed, precision=lax.Precision.HIGHEST)
    factor_low = jnp.linalg.cholesky(gram_mat)
    return lax.linalg.triangular_solve(factor_low, summed, left_side=False, lower=True, transpose_a=True)

def reference(gradients, errors, start_factors, moments, weights, vector_grads, vector_moments, vector_weights):
    mixed = gradients.astype(jnp.float32) + errors
    right_f = start_factors
    for round_idx in range(ROUNDS):
        summed = jnp.einsum('imkd,mdr->mkr', mixed, right_f, precision=lax.Precision.HIGHEST)
        basis_now = jax.vmap(orthonormal)(summed)
        right_f = jnp.einsum('imkd,mkr->mdr', mixed, basis_now, precision=lax.Precision.HIGHEST)
    approx = jnp.einsum('mkr,mdr->mkd', basis_now, right_f, precision=lax.Precision.HIGHEST) / REPLICAS
    new_errors = mixed - approx[None]
    new_moments = momentum_coef * moments + approx
    new_weights = (weights - step_rate * new_moments).astype(jnp.bfloat16)
    vector_mean = jnp.sum(vector_grads.astype(jnp.float32), axis=0) / REPLICAS
    new_vector_moments = momentum_coef * vector_moments + vector_mean
    new_vector_weights = vector_weights - step_rate * new_vector_moments
    return (new_errors, new_moments, new_weights, new_vector_moments, new_vector_weights)
```

```python
import functools

import jax
import jax.numpy as jnp
from jax import lax
from jax.experimental import pallas as pl
from jax.experimental.pallas import tpu as pltpu
from jax.sharding import PartitionSpec as P

ROUNDS = 2
LANES = 128
MESH = pl.DeviceIdType.MESH


momentum_coef = 0.9
step_rate = 0.1


def basis_from(gram_mat, summed):
    factor_low = jnp.linalg.cholesky(gram_mat)
    return lax.linalg.triangular_solve(
        factor_low, summed, left_side=False, lower=True, transpose_a=True
    )


def left_basis(mixed, right_f):
    partial_value = jnp.einsum("mkd,mdr->mkr", mixed, right_f, precision=lax.Precision.HIGHEST)
    summed = lax.psum(partial_value, ("dp", "tensor"))
    gram_mat = jnp.einsum("mkr,mks->mrs", summed, summed, precision=lax.Precision.HIGHEST)
    return basis_from(gram_mat, summed)


def update(mixed, start, moments, weights):
    right_f = start
    for round_idx in range(ROUNDS):
        basis_now = left_basis(mixed, right_f)
        right_part = jnp.einsum("mkd,mkr->mdr", mixed, basis_now, precision=lax.Precision.HIGHEST)
        right_f = lax.psum(right_part, "dp")
    replicas = lax.axis_size("dp")
    approx = (
        jnp.einsum("mkr,mdr->mkd", basis_now, right_f, precision=lax.Precision.HIGHEST) / replicas
    )
    fresh_errors = mixed - approx
    own_rows = moments.shape[1]
    my_rows = lax.dynamic_slice_in_dim(approx, lax.axis_index("dp") * own_rows, own_rows, 1)
    fresh_moments = momentum_coef * moments + my_rows
    fresh_weights = (weights - step_rate * fresh_moments).astype(jnp.bfloat16)
    regathered = lax.all_gather(fresh_weights, "dp", axis=1, tiled=True)
    return (fresh_errors, fresh_moments, regathered)


def per_device(
    gradients, errors, start_factors, moments, weights, vector_grads, vector_moments, vector_weights
):
    mixed = gradients[0].astype(jnp.float32) + errors[0]
    fresh_errors, fresh_moments, regathered = update(mixed, start_factors, moments, weights)
    vector_total = lax.psum(vector_grads[0].astype(jnp.float32), "dp")
    vector_mean = vector_total / lax.axis_size("dp")
    fresh_vector_moments = momentum_coef * vector_moments + vector_mean
    fresh_vector_weights = vector_weights - step_rate * fresh_vector_moments
    return (
        fresh_errors[None],
        fresh_moments,
        regathered,
        fresh_vector_moments,
        fresh_vector_weights,
    )


def split(x):
    high = x.astype(jnp.bfloat16)
    low = (x - high.astype(jnp.float32)).astype(jnp.bfloat16)
    return high, low


def product(x, high, low, dims):
    rows = x.shape[0]
    both = jnp.concatenate(split(x), axis=0)
    dot = functools.partial(
        lax.dot_general, dimension_numbers=(dims, ((), ())), preferred_element_type=jnp.float32
    )
    out = dot(both, high) + dot(both, low)
    return out[:rows] + out[rows:]


def exact_dot(x, y, dims):
    return lax.dot_general(
        x,
        y,
        (dims, ((), ())),
        precision=lax.Precision.HIGHEST,
        preferred_element_type=jnp.float32,
    )


def placed(x, at, rank):
    blocks = [jnp.zeros_like(x)] * (LANES // rank)
    blocks[at] = x
    return jnp.concatenate(blocks, axis=0)


def inverse_factors(sums, rank):
    row = lax.broadcasted_iota(jnp.int32, (rank, LANES), 0)
    lane = lax.broadcasted_iota(jnp.int32, (rank, LANES), 1)
    work = exact_dot(sums[0], placed(sums[0], 0, rank), ((1,), (1,)))
    work = work + exact_dot(sums[1], placed(sums[1], 2, rank), ((1,), (1,)))
    work = work + jnp.where((lane == row + rank) | (lane == row + 3 * rank), 1.0, 0.0)
    first = lane < 2 * rank
    single = lax.broadcasted_iota(jnp.int32, (rank, 1), 0)

    def eliminate(k, work):
        col0 = jnp.sum(jnp.where(lane == k, work, 0.0), axis=1, keepdims=True)
        col1 = jnp.sum(jnp.where(lane == k + 2 * rank, work, 0.0), axis=1, keepdims=True)
        pivot_row = jnp.sum(jnp.where(row == k, work, 0.0), axis=0, keepdims=True)
        here = single == k
        piv0 = jnp.sum(jnp.where(here, col0, 0.0), axis=0, keepdims=True)
        piv1 = jnp.sum(jnp.where(here, col1, 0.0), axis=0, keepdims=True)
        ratio = jnp.where(first, col0 / piv0, col1 / piv1)
        return work - jnp.where(row > k, ratio * pivot_row, 0.0)

    work = lax.fori_loop(0, rank, eliminate, work)
    diag0 = jnp.sum(jnp.where(lane == row, work, 0.0), axis=1, keepdims=True)
    diag1 = jnp.sum(jnp.where(lane == row + 2 * rank, work, 0.0), axis=1, keepdims=True)
    return work * jnp.where(first, 1.0 / jnp.sqrt(diag0), 1.0 / jnp.sqrt(diag1))


def kernel(
    nd,
    nt,
    rank,
    grad_ref,
    err_ref,
    start_ref,
    mom_ref,
    wgt_ref,
    vgrad_ref,
    vmom_ref,
    vwgt_ref,
    new_err_ref,
    new_mom_ref,
    new_wgt_ref,
    new_vmom_ref,
    new_vwgt_ref,
    high_ref,
    low_ref,
    left_part,
    left_in,
    left_mid,
    left_sum,
    right_part,
    right_in,
    right_sum,
    wgt_all,
    vec_all,
    approx_ref,
    t_send,
    t_recv,
    d_send,
    d_recv,
    bg_send,
    bg_recv,
):
    mats = high_ref.shape[0]
    d, t = lax.axis_index("dp"), lax.axis_index("tensor")
    dp_peers = [lax.rem(d + o, nd) for o in range(1, nd)]
    t_peers = [lax.rem(t + o, nt) for o in range(1, nt)]
    t_rows = left_in.shape[2]
    d_rows = right_in.shape[2]
    own = wgt_all.shape[2]

    barrier = pltpu.get_barrier_semaphore()
    for peer in dp_peers:
        pl.semaphore_signal(barrier, inc=1, device_id=(peer, t), device_id_type=MESH)
    for peer in t_peers:
        pl.semaphore_signal(barrier, inc=1, device_id=(d, peer), device_id_type=MESH)

    pending = []

    def push(src, dst, send, recv, device):
        copy = pltpu.make_async_remote_copy(
            src_ref=src,
            dst_ref=dst,
            send_sem=send,
            recv_sem=recv,
            device_id=device,
            device_id_type=MESH,
        )
        copy.start()
        pending.append(copy)
        return copy

    def rows_of(x, m):
        return x[m * rank : (m + 1) * rank]

    for m in range(mats):
        mixed = grad_ref[0, m].astype(jnp.float32) + err_ref[0, m]
        high, low = split(mixed)
        high_ref[m] = high
        low_ref[m] = low
    wgt_all[d] = wgt_ref[...] - (step_rate * momentum_coef) * mom_ref[...]
    vec_all[d] = vgrad_ref[0]
    right = [jnp.transpose(start_ref[m]) for m in range(mats)]

    background = []

    def push_background():
        o = len(background)
        if o < nd - 1:
            device = (dp_peers[o], t)
            background.append(
                push(wgt_all.at[d], wgt_all.at[d], bg_send.at[0, o], bg_recv.at[0, o], device)
            )

    vector_copies = []
    for rnd in range(ROUNDS):
        for m in range(mats):
            left_part[rnd, m * rank : (m + 1) * rank] = product(
                right[m], high_ref[m], low_ref[m], ((1,), (1,))
            )
        if rnd == 0:
            pl.semaphore_wait(barrier, nd - 1 + nt - 1)
        copies = [
            push(
                left_part.at[rnd, pl.ds(pl.multiple_of(peer * t_rows, t_rows), t_rows)],
                left_in.at[rnd, o],
                t_send.at[rnd, 0, o],
                t_recv.at[rnd, 0, o],
                (d, peer),
            )
            for o, peer in enumerate(t_peers)
        ]
        mine = pl.ds(pl.multiple_of(t * t_rows, t_rows), t_rows)
        total = left_part[rnd, mine]
        for o, copy in enumerate(copies):
            copy.wait_recv()
            total = total + left_in[rnd, o]
        left_mid[rnd, d] = total
        copies = [
            push(
                left_mid.at[rnd, d],
                left_mid.at[rnd, d],
                d_send.at[rnd, 0, o],
                d_recv.at[rnd, 0, o],
                (peer, t),
            )
            for o, peer in enumerate(dp_peers)
        ]
        if rnd == 0:
            vector_copies = [
                push(vgrad_ref.at[0], vec_all.at[d], bg_send.at[1, o], bg_recv.at[1, o], (peer, t))
                for o, peer in enumerate(dp_peers)
            ]
        push_background()
        for copy in copies:
            copy.wait_recv()
        total = left_mid[rnd, 0]
        for i in range(1, nd):
            total = total + left_mid[rnd, i]
        left_sum[rnd, mine] = total
        copies = [
            push(
                left_sum.at[rnd, mine],
                left_sum.at[rnd, mine],
                t_send.at[rnd, 1, o],
                t_recv.at[rnd, 1, o],
                (d, peer),
            )
            for o, peer in enumerate(t_peers)
        ]
        for copy in copies:
            copy.wait_recv()
        summed = left_sum[rnd]
        for m in range(mats):
            right_part[rnd, m * rank : (m + 1) * rank] = product(
                rows_of(summed, m), high_ref[m], low_ref[m], ((1,), (0,))
            )
        copies = [
            push(
                right_part.at[rnd, pl.ds(pl.multiple_of(peer * d_rows, d_rows), d_rows)],
                right_in.at[rnd, o],
                d_send.at[rnd, 1, o],
                d_recv.at[rnd, 1, o],
                (peer, t),
            )
            for o, peer in enumerate(dp_peers)
        ]
        push_background()
        push_background()
        inverse = inverse_factors([rows_of(summed, m) for m in range(mats)], rank)
        mine = pl.ds(pl.multiple_of(d * d_rows, d_rows), d_rows)
        total = right_part[rnd, mine]
        for o, copy in enumerate(copies):
            copy.wait_recv()
            total = total + right_in[rnd, o]
        right_sum[rnd, mine] = total
        copies = [
            push(
                right_sum.at[rnd, mine],
                right_sum.at[rnd, mine],
                d_send.at[rnd, 2, o],
                d_recv.at[rnd, 2, o],
                (peer, t),
            )
            for o, peer in enumerate(dp_peers)
        ]
        push_background()
        if rnd == ROUNDS - 1:
            basis = [
                exact_dot(inverse, placed(rows_of(summed, m), 2 * m + 1, rank), ((1,), (0,)))
                for m in range(mats)
            ]
            for copy in vector_copies:
                copy.wait_recv()
            vec_total = vec_all[0].astype(jnp.float32)
            for i in range(1, nd):
                vec_total = vec_total + vec_all[i].astype(jnp.float32)
            vmom = momentum_coef * vmom_ref[...] + vec_total * (1.0 / nd)
            new_vmom_ref[...] = vmom
            new_vwgt_ref[...] = vwgt_ref[...] - step_rate * vmom
        for copy in copies:
            copy.wait_recv()
        right_all = right_sum[rnd]
        right = [
            exact_dot(inverse, placed(rows_of(right_all, m), 2 * m + 1, rank), ((1,), (0,)))
            for m in range(mats)
        ]

    while len(background) < nd - 1:
        push_background()
    for m in range(mats):
        b_high, b_low = split(basis[m])
        r_high, r_low = split(right[m])
        approx = lax.dot_general(
            jnp.concatenate([b_high, b_high, b_low, b_low], axis=0),
            jnp.concatenate([r_high, r_low, r_high, r_low], axis=0),
            (((0,), (0,)), ((), ())),
            preferred_element_type=jnp.float32,
        ) * (1.0 / nd)
        approx_ref[m] = approx
        new_err_ref[0, m] = grad_ref[0, m].astype(jnp.float32) + err_ref[0, m] - approx
        own_rows = pl.ds(pl.multiple_of(d * own, own), own)
        new_mom_ref[m] = momentum_coef * mom_ref[m] + approx_ref[m, own_rows]
    for copy in background:
        copy.wait_recv()
    for m in range(mats):
        for i in range(nd):
            block = slice(i * own, (i + 1) * own)
            new_wgt_ref[m, block] = (wgt_all[i, m] - step_rate * approx_ref[m, block]).astype(
                jnp.bfloat16
            )
    for copy in pending:
        copy.wait_send()


def one_kernel(
    nd, nt, gradients, errors, start, moments, weights, vector_grads, vector_moments, vector_weights
):
    _, mats, rows, cols = gradients.shape
    rank = start.shape[2]
    vrows = vector_grads.shape[1]
    stack = mats * rank
    f32, bf16 = jnp.float32, jnp.bfloat16
    dma = pltpu.SemaphoreType.DMA
    vmem = pl.BlockSpec(memory_space=pltpu.VMEM)
    return pl.pallas_call(
        functools.partial(kernel, nd, nt, rank),
        out_shape=(
            jax.ShapeDtypeStruct(errors.shape, f32),
            jax.ShapeDtypeStruct(moments.shape, f32),
            jax.ShapeDtypeStruct((mats, rows, cols), bf16),
            jax.ShapeDtypeStruct(vector_moments.shape, f32),
            jax.ShapeDtypeStruct(vector_weights.shape, f32),
        ),
        in_specs=[vmem] * 8,
        out_specs=(vmem,) * 5,
        scratch_shapes=[
            pltpu.VMEM((mats, rows, cols), bf16),
            pltpu.VMEM((mats, rows, cols), bf16),
            pltpu.VMEM((ROUNDS, stack, rows), f32),
            pltpu.VMEM((ROUNDS, nt - 1, stack // nt, rows), f32),
            pltpu.VMEM((ROUNDS, nd, stack // nt, rows), f32),
            pltpu.VMEM((ROUNDS, stack, rows), f32),
            pltpu.VMEM((ROUNDS, stack, cols), f32),
            pltpu.VMEM((ROUNDS, nd - 1, stack // nd, cols), f32),
            pltpu.VMEM((ROUNDS, stack, cols), f32),
            pltpu.VMEM((nd, mats, rows // nd, cols), f32),
            pltpu.VMEM((nd, vrows, cols), bf16),
            pltpu.VMEM((mats, rows, cols), f32),
            dma((ROUNDS, 2, nt - 1)),
            dma((ROUNDS, 2, nt - 1)),
            dma((ROUNDS, 3, nd - 1)),
            dma((ROUNDS, 3, nd - 1)),
            dma((2, nd - 1)),
            dma((2, nd - 1)),
        ],
        compiler_params=pltpu.CompilerParams(
            collective_id=0, has_side_effects=True, vmem_limit_bytes=48 << 20
        ),
    )(gradients, errors, start, moments, weights, vector_grads, vector_moments, vector_weights)


def fits(nd, nt, mats, rows, rank):
    stack = mats * rank
    return (
        mats == 2
        and LANES == 4 * rank
        and nd > 1
        and nt > 1
        and stack % (8 * nt) == 0
        and stack % (8 * nd) == 0
        and rows % (16 * nd) == 0
    )


def dispatch(nd, nt, *args):
    gradients, start = args[0], args[2]
    if fits(nd, nt, gradients.shape[1], gradients.shape[2], start.shape[2]):
        return one_kernel(nd, nt, *args)
    return per_device(*args)


def solution(mesh):
    in_specs = (
        P("dp", None, None, "tensor"),
        P("dp", None, None, "tensor"),
        P(None, "tensor", None),
        P(None, "dp", "tensor"),
        P(None, "dp", "tensor"),
        P("dp", None, "tensor"),
        P(None, "tensor"),
        P(None, "tensor"),
    )
    out_specs = (
        P("dp", None, None, "tensor"),
        P(None, "dp", "tensor"),
        P(None, None, "tensor"),
        P(None, "tensor"),
        P(None, "tensor"),
    )
    return jax.shard_map(
        functools.partial(dispatch, mesh.shape["dp"], mesh.shape["tensor"]),
        mesh=mesh,
        in_specs=in_specs,
        out_specs=out_specs,
        check_vma=False,
    )
```

```python
import functools

import jax
import jax.numpy as jnp
from jax import lax
from jax.experimental import pallas as pl
from jax.experimental.pallas import tpu as pltpu
from jax.sharding import PartitionSpec as P

ROUNDS = 2
LANES = 128
MESH = pl.DeviceIdType.MESH


momentum_coef = 0.9
step_rate = 0.1


def basis_from(gram_mat, summed):
    factor_low = jnp.linalg.cholesky(gram_mat)
    return lax.linalg.triangular_solve(
        factor_low, summed, left_side=False, lower=True, transpose_a=True
    )


def left_basis(mixed, right_f):
    partial_value = jnp.einsum("mkd,mdr->mkr", mixed, right_f, precision=lax.Precision.HIGHEST)
    summed = lax.psum(partial_value, ("dp", "tensor"))
    gram_mat = jnp.einsum("mkr,mks->mrs", summed, summed, precision=lax.Precision.HIGHEST)
    return basis_from(gram_mat, summed)


def update(mixed, start, moments, weights):
    right_f = start
    for round_idx in range(ROUNDS):
        basis_now = left_basis(mixed, right_f)
        right_part = jnp.einsum("mkd,mkr->mdr", mixed, basis_now, precision=lax.Precision.HIGHEST)
        right_f = lax.psum(right_part, "dp")
    replicas = lax.axis_size("dp")
    approx = (
        jnp.einsum("mkr,mdr->mkd", basis_now, right_f, precision=lax.Precision.HIGHEST) / replicas
    )
    fresh_errors = mixed - approx
    own_rows = moments.shape[1]
    my_rows = lax.dynamic_slice_in_dim(approx, lax.axis_index("dp") * own_rows, own_rows, 1)
    fresh_moments = momentum_coef * moments + my_rows
    fresh_weights = (weights - step_rate * fresh_moments).astype(jnp.bfloat16)
    regathered = lax.all_gather(fresh_weights, "dp", axis=1, tiled=True)
    return (fresh_errors, fresh_moments, regathered)


def per_device(
    gradients, errors, start_factors, moments, weights, vector_grads, vector_moments, vector_weights
):
    mixed = gradients[0].astype(jnp.float32) + errors[0]
    fresh_errors, fresh_moments, regathered = update(mixed, start_factors, moments, weights)
    vector_total = lax.psum(vector_grads[0].astype(jnp.float32), "dp")
    vector_mean = vector_total / lax.axis_size("dp")
    fresh_vector_moments = momentum_coef * vector_moments + vector_mean
    fresh_vector_weights = vector_weights - step_rate * fresh_vector_moments
    return (
        fresh_errors[None],
        fresh_moments,
        regathered,
        fresh_vector_moments,
        fresh_vector_weights,
    )


def split(x):
    high = x.astype(jnp.bfloat16)
    low = (x - high.astype(jnp.float32)).astype(jnp.bfloat16)
    return high, low


def product(x, high, low, dims):
    rows = x.shape[0]
    both = jnp.concatenate(split(x), axis=0)
    dot = functools.partial(
        lax.dot_general, dimension_numbers=(dims, ((), ())), preferred_element_type=jnp.float32
    )
    out = dot(both, high) + dot(both, low)
    return out[:rows] + out[rows:]


def exact_dot(x, y, dims):
    return lax.dot_general(
        x,
        y,
        (dims, ((), ())),
        precision=lax.Precision.HIGHEST,
        preferred_element_type=jnp.float32,
    )


def placed(x, at, rank):
    blocks = [jnp.zeros_like(x)] * (LANES // rank)
    blocks[at] = x
    return jnp.concatenate(blocks, axis=0)


def inverse_factors(sums, rank):
    row = lax.broadcasted_iota(jnp.int32, (rank, LANES), 0)
    lane = lax.broadcasted_iota(jnp.int32, (rank, LANES), 1)
    work = exact_dot(sums[0], placed(sums[0], 0, rank), ((1,), (1,)))
    work = work + exact_dot(sums[1], placed(sums[1], 2, rank), ((1,), (1,)))
    work = work + jnp.where((lane == row + rank) | (lane == row + 3 * rank), 1.0, 0.0)
    first = lane < 2 * rank
    single = lax.broadcasted_iota(jnp.int32, (rank, 1), 0)

    def eliminate(k, work):
        col0 = jnp.sum(jnp.where(lane == k, work, 0.0), axis=1, keepdims=True)
        col1 = jnp.sum(jnp.where(lane == k + 2 * rank, work, 0.0), axis=1, keepdims=True)
        pivot_row = jnp.sum(jnp.where(row == k, work, 0.0), axis=0, keepdims=True)
        here = single == k
        piv0 = jnp.sum(jnp.where(here, col0, 0.0), axis=0, keepdims=True)
        piv1 = jnp.sum(jnp.where(here, col1, 0.0), axis=0, keepdims=True)
        ratio = jnp.where(first, col0 / piv0, col1 / piv1)
        return work - jnp.where(row > k, ratio * pivot_row, 0.0)

    work = lax.fori_loop(0, rank, eliminate, work)
    diag0 = jnp.sum(jnp.where(lane == row, work, 0.0), axis=1, keepdims=True)
    diag1 = jnp.sum(jnp.where(lane == row + 2 * rank, work, 0.0), axis=1, keepdims=True)
    return work * jnp.where(first, 1.0 / jnp.sqrt(diag0), 1.0 / jnp.sqrt(diag1))


def reduce_kernel(
    nd,
    nt,
    rank,
    grad_ref,
    err_ref,
    start_ref,
    mom_ref,
    wgt_ref,
    vgrad_ref,
    basis_ref,
    right_ref,
    wgt_t_ref,
    vec_ref,
    high_ref,
    low_ref,
    left_part,
    left_in,
    left_mid,
    left_sum,
    right_part,
    right_in,
    right_sum,
    wgt_all,
    vec_all,
    t_send,
    t_recv,
    d_send,
    d_recv,
    w_send,
    w_recv,
    v_send,
    v_recv,
):
    mats = high_ref.shape[0]
    rows = high_ref.shape[2]
    d, t = lax.axis_index("dp"), lax.axis_index("tensor")
    dp_peers = [lax.rem(d + o, nd) for o in range(1, nd)]
    t_peers = [lax.rem(t + o, nt) for o in range(1, nt)]
    t_rows = left_in.shape[2]
    d_rows = right_in.shape[2]
    pairs = nd // 2
    high_at, low_at = d // 2, lax.rem(d, 2)
    partner = high_at * 2 + 1 - low_at

    barrier = pltpu.get_barrier_semaphore()
    for peer in dp_peers:
        pl.semaphore_signal(barrier, inc=1, device_id=(peer, t), device_id_type=MESH)
    for peer in t_peers:
        pl.semaphore_signal(barrier, inc=1, device_id=(d, peer), device_id_type=MESH)

    pending = []

    def push(src, dst, send, recv, device):
        copy = pltpu.make_async_remote_copy(
            src_ref=src,
            dst_ref=dst,
            send_sem=send,
            recv_sem=recv,
            device_id=device,
            device_id_type=MESH,
        )
        copy.start()
        pending.append(copy)
        return copy

    def rows_of(x, m):
        return x[m * rank : (m + 1) * rank]

    for m in range(mats):
        mixed = grad_ref[0, m].astype(jnp.float32) + err_ref[0, m]
        high, low = split(mixed)
        high_ref[m] = high
        low_ref[m] = low
    right = [start_ref[m] for m in range(mats)]

    offsets = sorted(range(1, pairs), key=lambda o: min(o, pairs - o))
    straight, relayed = [], []

    def push_block(block, sem, device):
        return push(
            wgt_all.at[block], wgt_all.at[block], w_send.at[sem], w_recv.at[sem], (device, t)
        )

    def push_weights(window):
        if window == 0:
            relayed.append(push_block(d, 0, partner))
        if window < len(offsets):
            o = offsets[window]
            to = lax.rem(high_at + o, pairs) * 2 + low_at
            straight.append(push_block(d, 2 * window + 1, to))
        if 1 <= window <= len(offsets):
            o = offsets[window - 1]
            block = lax.rem(high_at + pairs - o, pairs) * 2 + low_at
            straight[window - 1].wait_recv()
            relayed.append(push_block(block, 2 * window, partner))

    for rnd in range(ROUNDS):
        for m in range(mats):
            left_part[rnd, m * rank : (m + 1) * rank] = product(
                right[m], high_ref[m], low_ref[m], ((1,), (0,))
            )
        if rnd == 0:
            pl.semaphore_wait(barrier, nd - 1 + nt - 1)
        copies = [
            push(
                left_part.at[rnd, pl.ds(pl.multiple_of(peer * t_rows, t_rows), t_rows)],
                left_in.at[rnd, o],
                t_send.at[rnd, 0, o],
                t_recv.at[rnd, 0, o],
                (d, peer),
            )
            for o, peer in enumerate(t_peers)
        ]
        if rnd == 0:
            wgt_all[d] = wgt_ref[...] - (step_rate * momentum_coef) * mom_ref[...]
            vec_all[d] = vgrad_ref[0]
        push_weights(2 * rnd)
        mine = pl.ds(pl.multiple_of(t * t_rows, t_rows), t_rows)
        total = left_part[rnd, mine]
        for o, copy in enumerate(copies):
            copy.wait_recv()
            total = total + left_in[rnd, o]
        left_mid[rnd, d] = total
        copies = [
            push(
                left_mid.at[rnd, d],
                left_mid.at[rnd, d],
                d_send.at[rnd, 0, o],
                d_recv.at[rnd, 0, o],
                (peer, t),
            )
            for o, peer in enumerate(dp_peers)
        ]
        for copy in copies:
            copy.wait_recv()
        total = left_mid[rnd, 0]
        for i in range(1, nd):
            total = total + left_mid[rnd, i]
        left_sum[rnd, mine] = total
        copies = [
            push(
                left_sum.at[rnd, mine],
                left_sum.at[rnd, mine],
                t_send.at[rnd, 1, o],
                t_recv.at[rnd, 1, o],
                (d, peer),
            )
            for o, peer in enumerate(t_peers)
        ]
        push_weights(2 * rnd + 1)
        if rnd == ROUNDS - 1:
            vector_copies = [
                push(vgrad_ref.at[0], vec_all.at[d], v_send.at[o], v_recv.at[o], (peer, t))
                for o, peer in enumerate(dp_peers)
            ]
        for copy in copies:
            copy.wait_recv()
        summed = left_sum[rnd]
        for m in range(mats):
            right_part[rnd, m * rank : (m + 1) * rank] = product(
                rows_of(summed, m), high_ref[m], low_ref[m], ((1,), (1,))
            )
        copies = [
            push(
                right_part.at[rnd, pl.ds(pl.multiple_of(peer * d_rows, d_rows), d_rows)],
                right_in.at[rnd, o],
                d_send.at[rnd, 1, o],
                d_recv.at[rnd, 1, o],
                (peer, t),
            )
            for o, peer in enumerate(dp_peers)
        ]
        inverse = inverse_factors([rows_of(summed, m) for m in range(mats)], rank)
        mine = pl.ds(pl.multiple_of(d * d_rows, d_rows), d_rows)
        total = right_part[rnd, mine]
        for o, copy in enumerate(copies):
            copy.wait_recv()
            total = total + right_in[rnd, o]
        right_sum[rnd, mine] = total
        copies = [
            push(
                right_sum.at[rnd, mine],
                right_sum.at[rnd, mine],
                d_send.at[rnd, 2, o],
                d_recv.at[rnd, 2, o],
                (peer, t),
            )
            for o, peer in enumerate(dp_peers)
        ]
        if rnd == ROUNDS - 1:
            for m in range(mats):
                basis_ref[m * rank : (m + 1) * rank] = exact_dot(
                    inverse, placed(rows_of(summed, m), 2 * m + 1, rank), ((1,), (0,))
                )
            for copy in vector_copies:
                copy.wait_recv()
            vec_total = vec_all[0].astype(jnp.float32)
            for i in range(1, nd):
                vec_total = vec_total + vec_all[i].astype(jnp.float32)
            vec_ref[...] = vec_total
            for window in range(2 * ROUNDS, len(offsets) + 1):
                push_weights(window)
            for copy in relayed:
                copy.wait_recv()
            for m in range(mats):
                whole = jnp.concatenate([wgt_all[i, m] for i in range(nd)], axis=0)
                wgt_t_ref[m] = jnp.transpose(whole)
        for copy in copies:
            copy.wait_recv()
        right_all = right_sum[rnd]
        right = [
            exact_dot(inverse, placed(rows_of(right_all, m), 2 * m + 1, rank), ((1,), (0,)))
            for m in range(mats)
        ]
    for m in range(mats):
        right_ref[m * rank : (m + 1) * rank] = right[m]
    for copy in pending:
        copy.wait_send()


def apply_kernel(
    nd,
    rank,
    grad_ref,
    err_ref,
    basis_ref,
    right_ref,
    wgt_t_ref,
    vec_ref,
    mom_ref,
    vmom_ref,
    vwgt_ref,
    new_err_ref,
    new_mom_ref,
    new_wgt_ref,
    new_vmom_ref,
    new_vwgt_ref,
):
    mats, own = mom_ref.shape[0], mom_ref.shape[1]
    rows = basis_ref.shape[1]
    d = lax.axis_index("dp")
    row = lax.broadcasted_iota(jnp.int32, (own, rows), 0)
    lane = lax.broadcasted_iota(jnp.int32, (own, rows), 1)
    select = jnp.where(lane == row + d * own, 1.0, 0.0).astype(jnp.bfloat16)
    dot = functools.partial(lax.dot_general, preferred_element_type=jnp.float32)
    vmom = momentum_coef * vmom_ref[...] + vec_ref[...] * (1.0 / nd)
    new_vmom_ref[...] = vmom
    new_vwgt_ref[...] = vwgt_ref[...] - step_rate * vmom
    for m in range(mats):
        b_high, b_low = split(basis_ref[m * rank : (m + 1) * rank])
        r_high, r_low = split(right_ref[m * rank : (m + 1) * rank])
        b_all = jnp.concatenate([b_high, b_high, b_low, b_low], axis=0)
        r_all = jnp.concatenate([r_high, r_low, r_high, r_low], axis=0)
        approx = dot(r_all, b_all, (((0,), (0,)), ((), ()))) * (1.0 / nd)
        new_err_ref[0, m] = grad_ref[0, m].astype(jnp.float32) + err_ref[0, m] - approx
        new_wgt_ref[m] = (wgt_t_ref[m] - step_rate * approx).astype(jnp.bfloat16)
        b_own = dot(select, b_all, (((1,), (1,)), ((), ()))).astype(jnp.bfloat16)
        approx_own = dot(b_own, r_all, (((1,), (0,)), ((), ()))) * (1.0 / nd)
        new_mom_ref[m] = momentum_coef * mom_ref[m] + approx_own


def two_kernels(
    nd, nt, gradients, errors, start, moments, weights, vector_grads, vector_moments, vector_weights
):
    _, mats, rows, cols = gradients.shape
    rank = start.shape[2]
    vrows = vector_grads.shape[1]
    stack = mats * rank
    f32, bf16 = jnp.float32, jnp.bfloat16
    dma = pltpu.SemaphoreType.DMA
    vmem = pl.BlockSpec(memory_space=pltpu.VMEM)
    grads_t = jnp.swapaxes(gradients, 2, 3)
    errors_t = jnp.swapaxes(errors, 2, 3)
    basis, right, weights_t, vector_sum = pl.pallas_call(
        functools.partial(reduce_kernel, nd, nt, rank),
        out_shape=(
            jax.ShapeDtypeStruct((stack, rows), f32),
            jax.ShapeDtypeStruct((stack, cols), f32),
            jax.ShapeDtypeStruct((mats, cols, rows), f32),
            jax.ShapeDtypeStruct((vrows, cols), f32),
        ),
        in_specs=[vmem] * 6,
        out_specs=(vmem,) * 4,
        scratch_shapes=[
            pltpu.VMEM((mats, cols, rows), bf16),
            pltpu.VMEM((mats, cols, rows), bf16),
            pltpu.VMEM((ROUNDS, stack, rows), f32),
            pltpu.VMEM((ROUNDS, nt - 1, stack // nt, rows), f32),
            pltpu.VMEM((ROUNDS, nd, stack // nt, rows), f32),
            pltpu.VMEM((ROUNDS, stack, rows), f32),
            pltpu.VMEM((ROUNDS, stack, cols), f32),
            pltpu.VMEM((ROUNDS, nd - 1, stack // nd, cols), f32),
            pltpu.VMEM((ROUNDS, stack, cols), f32),
            pltpu.VMEM((nd, mats, rows // nd, cols), f32),
            pltpu.VMEM((nd, vrows, cols), bf16),
            dma((ROUNDS, 2, nt - 1)),
            dma((ROUNDS, 2, nt - 1)),
            dma((ROUNDS, 3, nd - 1)),
            dma((ROUNDS, 3, nd - 1)),
            dma((nd - 1,)),
            dma((nd - 1,)),
            dma((nd - 1,)),
            dma((nd - 1,)),
        ],
        compiler_params=pltpu.CompilerParams(
            collective_id=0, has_side_effects=True, vmem_limit_bytes=32 << 20
        ),
    )(grads_t, errors_t, jnp.swapaxes(start, 1, 2), moments, weights, vector_grads)
    new_errors, new_moments, new_weights, new_vmom, new_vwgt = pl.pallas_call(
        functools.partial(apply_kernel, nd, rank),
        out_shape=(
            jax.ShapeDtypeStruct(errors_t.shape, f32),
            jax.ShapeDtypeStruct(moments.shape, f32),
            jax.ShapeDtypeStruct((mats, cols, rows), bf16),
            jax.ShapeDtypeStruct(vector_moments.shape, f32),
            jax.ShapeDtypeStruct(vector_weights.shape, f32),
        ),
        in_specs=[vmem] * 9,
        out_specs=(vmem,) * 5,
        compiler_params=pltpu.CompilerParams(vmem_limit_bytes=32 << 20),
    )(
        grads_t,
        errors_t,
        basis,
        right,
        weights_t,
        vector_sum,
        moments,
        vector_moments,
        vector_weights,
    )
    return (
        jnp.swapaxes(new_errors, 2, 3),
        new_moments,
        jnp.swapaxes(new_weights, 1, 2),
        new_vmom,
        new_vwgt,
    )


def fits(nd, nt, mats, rows, rank):
    stack = mats * rank
    return (
        mats == 2
        and LANES == 4 * rank
        and nd % 2 == 0
        and nt > 1
        and stack % (8 * nt) == 0
        and stack % (8 * nd) == 0
        and rows % (8 * nd) == 0
    )


def dispatch(nd, nt, *args):
    gradients, start = args[0], args[2]
    if fits(nd, nt, gradients.shape[1], gradients.shape[2], start.shape[2]):
        return two_kernels(nd, nt, *args)
    return per_device(*args)


def solution(mesh):
    in_specs = (
        P("dp", None, None, "tensor"),
        P("dp", None, None, "tensor"),
        P(None, "tensor", None),
        P(None, "dp", "tensor"),
        P(None, "dp", "tensor"),
        P("dp", None, "tensor"),
        P(None, "tensor"),
        P(None, "tensor"),
    )
    out_specs = (
        P("dp", None, None, "tensor"),
        P(None, "dp", "tensor"),
        P(None, None, "tensor"),
        P(None, "tensor"),
        P(None, "tensor"),
    )
    return jax.shard_map(
        functools.partial(dispatch, mesh.shape["dp"], mesh.shape["tensor"]),
        mesh=mesh,
        in_specs=in_specs,
        out_specs=out_specs,
        check_vma=False,
    )
```

```python
import functools

import jax
import jax.numpy as jnp
from jax import lax
from jax.experimental import pallas as pl
from jax.experimental.pallas import tpu as pltpu
from jax.sharding import PartitionSpec as P

ROUNDS = 2
LANES = 128
MESH = pl.DeviceIdType.MESH


momentum_coef = 0.9
step_rate = 0.1


def basis_from(gram_mat, summed):
    factor_low = jnp.linalg.cholesky(gram_mat)
    return lax.linalg.triangular_solve(
        factor_low, summed, left_side=False, lower=True, transpose_a=True
    )


def left_basis(mixed, right_f):
    partial_value = jnp.einsum("mkd,mdr->mkr", mixed, right_f, precision=lax.Precision.HIGHEST)
    summed = lax.psum(partial_value, ("dp", "tensor"))
    gram_mat = jnp.einsum("mkr,mks->mrs", summed, summed, precision=lax.Precision.HIGHEST)
    return basis_from(gram_mat, summed)


def update(mixed, start, moments, weights):
    right_f = start
    for round_idx in range(ROUNDS):
        basis_now = left_basis(mixed, right_f)
        right_part = jnp.einsum("mkd,mkr->mdr", mixed, basis_now, precision=lax.Precision.HIGHEST)
        right_f = lax.psum(right_part, "dp")
    replicas = lax.axis_size("dp")
    approx = (
        jnp.einsum("mkr,mdr->mkd", basis_now, right_f, precision=lax.Precision.HIGHEST) / replicas
    )
    fresh_errors = mixed - approx
    own_rows = moments.shape[1]
    my_rows = lax.dynamic_slice_in_dim(approx, lax.axis_index("dp") * own_rows, own_rows, 1)
    fresh_moments = momentum_coef * moments + my_rows
    fresh_weights = (weights - step_rate * fresh_moments).astype(jnp.bfloat16)
    regathered = lax.all_gather(fresh_weights, "dp", axis=1, tiled=True)
    return (fresh_errors, fresh_moments, regathered)


def per_device(
    gradients, errors, start_factors, moments, weights, vector_grads, vector_moments, vector_weights
):
    mixed = gradients[0].astype(jnp.float32) + errors[0]
    fresh_errors, fresh_moments, regathered = update(mixed, start_factors, moments, weights)
    vector_total = lax.psum(vector_grads[0].astype(jnp.float32), "dp")
    vector_mean = vector_total / lax.axis_size("dp")
    fresh_vector_moments = momentum_coef * vector_moments + vector_mean
    fresh_vector_weights = vector_weights - step_rate * fresh_vector_moments
    return (
        fresh_errors[None],
        fresh_moments,
        regathered,
        fresh_vector_moments,
        fresh_vector_weights,
    )


def split(x):
    high = x.astype(jnp.bfloat16)
    low = (x - high.astype(jnp.float32)).astype(jnp.bfloat16)
    return high, low


def product(x, high, low, dims):
    rows = x.shape[0]
    both = jnp.concatenate(split(x), axis=0)
    dot = functools.partial(
        lax.dot_general, dimension_numbers=(dims, ((), ())), preferred_element_type=jnp.float32
    )
    out = dot(both, high) + dot(both, low)
    return out[:rows] + out[rows:]


def exact_dot(x, y, dims):
    return lax.dot_general(
        x,
        y,
        (dims, ((), ())),
        precision=lax.Precision.HIGHEST,
        preferred_element_type=jnp.float32,
    )


def placed(x, at, rank):
    blocks = [jnp.zeros_like(x)] * (LANES // rank)
    blocks[at] = x
    return jnp.concatenate(blocks, axis=0)


def inverse_factors(sums, rank):
    row = lax.broadcasted_iota(jnp.int32, (rank, LANES), 0)
    lane = lax.broadcasted_iota(jnp.int32, (rank, LANES), 1)
    work = exact_dot(sums[0], placed(sums[0], 0, rank), ((1,), (1,)))
    work = work + exact_dot(sums[1], placed(sums[1], 2, rank), ((1,), (1,)))
    work = work + jnp.where((lane == row + rank) | (lane == row + 3 * rank), 1.0, 0.0)
    first = lane < 2 * rank
    single = lax.broadcasted_iota(jnp.int32, (rank, 1), 0)

    def eliminate(k, work):
        col0 = jnp.sum(jnp.where(lane == k, work, 0.0), axis=1, keepdims=True)
        col1 = jnp.sum(jnp.where(lane == k + 2 * rank, work, 0.0), axis=1, keepdims=True)
        pivot_row = jnp.sum(jnp.where(row == k, work, 0.0), axis=0, keepdims=True)
        here = single == k
        piv0 = jnp.sum(jnp.where(here, col0, 0.0), axis=0, keepdims=True)
        piv1 = jnp.sum(jnp.where(here, col1, 0.0), axis=0, keepdims=True)
        ratio = jnp.where(first, col0 / piv0, col1 / piv1)
        return work - jnp.where(row > k, ratio * pivot_row, 0.0)

    work = lax.fori_loop(0, rank, eliminate, work)
    diag0 = jnp.sum(jnp.where(lane == row, work, 0.0), axis=1, keepdims=True)
    diag1 = jnp.sum(jnp.where(lane == row + 2 * rank, work, 0.0), axis=1, keepdims=True)
    return work * jnp.where(first, 1.0 / jnp.sqrt(diag0), 1.0 / jnp.sqrt(diag1))


def reduce_kernel(
    nd,
    nt,
    rank,
    grad_hbm,
    err_hbm,
    start_hbm,
    mom_hbm,
    wgt_hbm,
    vgrad_hbm,
    basis_ref,
    right_ref,
    wgt_t_ref,
    vec_ref,
    grad_ref,
    err_ref,
    start_ref,
    mom_ref,
    wgt_ref,
    high_ref,
    low_ref,
    high_t_ref,
    low_t_ref,
    left_part,
    left_in,
    left_mid,
    left_sum,
    right_part,
    right_in,
    right_sum,
    wgt_all,
    vec_all,
    t_send,
    t_recv,
    d_send,
    d_recv,
    w_send,
    w_recv,
    v_send,
    v_recv,
    load_sem,
):
    mats = high_ref.shape[0]
    rows = high_ref.shape[2]
    d, t = lax.axis_index("dp"), lax.axis_index("tensor")
    dp_peers = [lax.rem(d + o, nd) for o in range(1, nd)]
    t_peers = [lax.rem(t + o, nt) for o in range(1, nt)]
    t_rows = left_in.shape[2]
    d_rows = right_in.shape[2]
    pairs = nd // 2
    high_at, low_at = d // 2, lax.rem(d, 2)
    partner = high_at * 2 + 1 - low_at

    barrier = pltpu.get_barrier_semaphore()
    for peer in dp_peers:
        pl.semaphore_signal(barrier, inc=1, device_id=(peer, t), device_id_type=MESH)
    for peer in t_peers:
        pl.semaphore_signal(barrier, inc=1, device_id=(d, peer), device_id_type=MESH)

    loads = []
    for m in range(mats):
        loads.append((start_hbm.at[m], start_ref.at[m]))
        loads.append((grad_hbm.at[0, m], grad_ref.at[m]))
        loads.append((err_hbm.at[0, m], err_ref.at[m]))
    loads += [(mom_hbm, mom_ref), (wgt_hbm, wgt_ref), (vgrad_hbm.at[0], vec_all.at[d])]
    loads = [
        pltpu.make_async_copy(src, dst, load_sem.at[i]) for i, (src, dst) in enumerate(loads)
    ]
    for load in loads:
        load.start()

    pending = []

    def push(src, dst, send, recv, device):
        copy = pltpu.make_async_remote_copy(
            src_ref=src,
            dst_ref=dst,
            send_sem=send,
            recv_sem=recv,
            device_id=device,
            device_id_type=MESH,
        )
        copy.start()
        pending.append(copy)
        return copy

    def rows_of(x, m):
        return x[m * rank : (m + 1) * rank]

    right = []
    for m in range(mats):
        for load in loads[3 * m : 3 * m + 3]:
            load.wait()
        mixed = grad_ref[m].astype(jnp.float32) + err_ref[m]
        high, low = split(mixed)
        high_ref[m] = high
        low_ref[m] = low
        right.append(start_ref[m])

    offsets = sorted(range(1, pairs), key=lambda o: min(o, pairs - o))
    straight, relayed = [], []

    def push_block(block, sem, device):
        return push(
            wgt_all.at[block], wgt_all.at[block], w_send.at[sem], w_recv.at[sem], (device, t)
        )

    def push_weights(window):
        if window == 0:
            relayed.append(push_block(d, 0, partner))
        if window < len(offsets):
            o = offsets[window]
            to = lax.rem(high_at + o, pairs) * 2 + low_at
            straight.append(push_block(d, 2 * window + 1, to))
        if 1 <= window <= len(offsets):
            o = offsets[window - 1]
            block = lax.rem(high_at + pairs - o, pairs) * 2 + low_at
            straight[window - 1].wait_recv()
            relayed.append(push_block(block, 2 * window, partner))

    for rnd in range(ROUNDS):
        for m in range(mats):
            left_part[rnd, m * rank : (m + 1) * rank] = product(
                right[m], high_ref[m], low_ref[m], ((1,), (0,))
            )
        if rnd == 0:
            pl.semaphore_wait(barrier, nd - 1 + nt - 1)
        copies = [
            push(
                left_part.at[rnd, pl.ds(pl.multiple_of(peer * t_rows, t_rows), t_rows)],
                left_in.at[rnd, o],
                t_send.at[rnd, 0, o],
                t_recv.at[rnd, 0, o],
                (d, peer),
            )
            for o, peer in enumerate(t_peers)
        ]
        if rnd == 0:
            for load in loads[3 * mats :]:
                load.wait()
            wgt_all[d] = wgt_ref[...] - (step_rate * momentum_coef) * mom_ref[...]
        push_weights(2 * rnd)
        if rnd == 0:
            for m in range(mats):
                high_t_ref[m] = jnp.transpose(high_ref[m])
                low_t_ref[m] = jnp.transpose(low_ref[m])
        mine = pl.ds(pl.multiple_of(t * t_rows, t_rows), t_rows)
        total = left_part[rnd, mine]
        for o, copy in enumerate(copies):
            copy.wait_recv()
            total = total + left_in[rnd, o]
        left_mid[rnd, d] = total
        copies = [
            push(
                left_mid.at[rnd, d],
                left_mid.at[rnd, d],
                d_send.at[rnd, 0, o],
                d_recv.at[rnd, 0, o],
                (peer, t),
            )
            for o, peer in enumerate(dp_peers)
        ]
        for copy in copies:
            copy.wait_recv()
        total = left_mid[rnd, 0]
        for i in range(1, nd):
            total = total + left_mid[rnd, i]
        left_sum[rnd, mine] = total
        copies = [
            push(
                left_sum.at[rnd, mine],
                left_sum.at[rnd, mine],
                t_send.at[rnd, 1, o],
                t_recv.at[rnd, 1, o],
                (d, peer),
            )
            for o, peer in enumerate(t_peers)
        ]
        push_weights(2 * rnd + 1)
        if rnd == ROUNDS - 1:
            vector_copies = [
                push(vec_all.at[d], vec_all.at[d], v_send.at[o], v_recv.at[o], (peer, t))
                for o, peer in enumerate(dp_peers)
            ]
        for copy in copies:
            copy.wait_recv()
        summed = left_sum[rnd]
        for m in range(mats):
            right_part[rnd, m * rank : (m + 1) * rank] = product(
                rows_of(summed, m), high_t_ref[m], low_t_ref[m], ((1,), (0,))
            )
        copies = [
            push(
                right_part.at[rnd, pl.ds(pl.multiple_of(peer * d_rows, d_rows), d_rows)],
                right_in.at[rnd, o],
                d_send.at[rnd, 1, o],
                d_recv.at[rnd, 1, o],
                (peer, t),
            )
            for o, peer in enumerate(dp_peers)
        ]
        inverse = inverse_factors([rows_of(summed, m) for m in range(mats)], rank)
        mine = pl.ds(pl.multiple_of(d * d_rows, d_rows), d_rows)
        total = right_part[rnd, mine]
        for o, copy in enumerate(copies):
            copy.wait_recv()
            total = total + right_in[rnd, o]
        right_sum[rnd, mine] = total
        copies = [
            push(
                right_sum.at[rnd, mine],
                right_sum.at[rnd, mine],
                d_send.at[rnd, 2, o],
                d_recv.at[rnd, 2, o],
                (peer, t),
            )
            for o, peer in enumerate(dp_peers)
        ]
        if rnd == ROUNDS - 1:
            for m in range(mats):
                basis_ref[m * rank : (m + 1) * rank] = exact_dot(
                    inverse, placed(rows_of(summed, m), 2 * m + 1, rank), ((1,), (0,))
                )
            for copy in vector_copies:
                copy.wait_recv()
            vec_total = vec_all[0].astype(jnp.float32)
            for i in range(1, nd):
                vec_total = vec_total + vec_all[i].astype(jnp.float32)
            vec_ref[...] = vec_total
            for window in range(2 * ROUNDS, len(offsets) + 1):
                push_weights(window)
            for copy in relayed:
                copy.wait_recv()
            for m in range(mats):
                whole = jnp.concatenate([wgt_all[i, m] for i in range(nd)], axis=0)
                wgt_t_ref[m] = jnp.transpose(whole)
        for copy in copies:
            copy.wait_recv()
        right_all = right_sum[rnd]
        right = [
            exact_dot(inverse, placed(rows_of(right_all, m), 2 * m + 1, rank), ((1,), (0,)))
            for m in range(mats)
        ]
    for m in range(mats):
        right_ref[m * rank : (m + 1) * rank] = right[m]
    for copy in pending:
        copy.wait_send()


def apply_kernel(
    nd,
    rank,
    grad_ref,
    err_ref,
    basis_ref,
    right_ref,
    wgt_t_ref,
    vec_ref,
    mom_ref,
    vmom_ref,
    vwgt_ref,
    new_err_ref,
    new_mom_ref,
    new_wgt_ref,
    new_vmom_ref,
    new_vwgt_ref,
):
    mats, own = mom_ref.shape[0], mom_ref.shape[1]
    rows = basis_ref.shape[1]
    d = lax.axis_index("dp")
    row = lax.broadcasted_iota(jnp.int32, (own, rows), 0)
    lane = lax.broadcasted_iota(jnp.int32, (own, rows), 1)
    select = jnp.where(lane == row + d * own, 1.0, 0.0).astype(jnp.bfloat16)
    dot = functools.partial(lax.dot_general, preferred_element_type=jnp.float32)
    vmom = momentum_coef * vmom_ref[...] + vec_ref[...] * (1.0 / nd)
    new_vmom_ref[...] = vmom
    new_vwgt_ref[...] = vwgt_ref[...] - step_rate * vmom
    for m in range(mats):
        b_high, b_low = split(basis_ref[m * rank : (m + 1) * rank])
        r_high, r_low = split(right_ref[m * rank : (m + 1) * rank])
        b_all = jnp.concatenate([b_high, b_high, b_low, b_low], axis=0)
        r_all = jnp.concatenate([r_high, r_low, r_high, r_low], axis=0)
        approx = dot(r_all, b_all, (((0,), (0,)), ((), ()))) * (1.0 / nd)
        new_err_ref[0, m] = grad_ref[0, m].astype(jnp.float32) + err_ref[0, m] - approx
        new_wgt_ref[m] = (wgt_t_ref[m] - step_rate * approx).astype(jnp.bfloat16)
        b_own = dot(select, b_all, (((1,), (1,)), ((), ()))).astype(jnp.bfloat16)
        approx_own = dot(b_own, r_all, (((1,), (0,)), ((), ()))) * (1.0 / nd)
        new_mom_ref[m] = momentum_coef * mom_ref[m] + approx_own


def two_kernels(
    nd, nt, gradients, errors, start, moments, weights, vector_grads, vector_moments, vector_weights
):
    _, mats, rows, cols = gradients.shape
    rank = start.shape[2]
    vrows = vector_grads.shape[1]
    stack = mats * rank
    f32, bf16 = jnp.float32, jnp.bfloat16
    dma = pltpu.SemaphoreType.DMA
    vmem = pl.BlockSpec(memory_space=pltpu.VMEM)
    hbm = pl.BlockSpec(memory_space=pltpu.HBM)
    grads_t = jnp.swapaxes(gradients, 2, 3)
    errors_t = jnp.swapaxes(errors, 2, 3)
    basis, right, weights_t, vector_sum = pl.pallas_call(
        functools.partial(reduce_kernel, nd, nt, rank),
        out_shape=(
            jax.ShapeDtypeStruct((stack, rows), f32),
            jax.ShapeDtypeStruct((stack, cols), f32),
            jax.ShapeDtypeStruct((mats, cols, rows), f32),
            jax.ShapeDtypeStruct((vrows, cols), f32),
        ),
        in_specs=[hbm] * 6,
        out_specs=(vmem,) * 4,
        scratch_shapes=[
            pltpu.VMEM((mats, cols, rows), bf16),
            pltpu.VMEM((mats, cols, rows), f32),
            pltpu.VMEM((mats, rank, cols), f32),
            pltpu.VMEM(moments.shape, f32),
            pltpu.VMEM(moments.shape, f32),
            pltpu.VMEM((mats, cols, rows), bf16),
            pltpu.VMEM((mats, cols, rows), bf16),
            pltpu.VMEM((mats, rows, cols), bf16),
            pltpu.VMEM((mats, rows, cols), bf16),
            pltpu.VMEM((ROUNDS, stack, rows), f32),
            pltpu.VMEM((ROUNDS, nt - 1, stack // nt, rows), f32),
            pltpu.VMEM((ROUNDS, nd, stack // nt, rows), f32),
            pltpu.VMEM((ROUNDS, stack, rows), f32),
            pltpu.VMEM((ROUNDS, stack, cols), f32),
            pltpu.VMEM((ROUNDS, nd - 1, stack // nd, cols), f32),
            pltpu.VMEM((ROUNDS, stack, cols), f32),
            pltpu.VMEM((nd, mats, rows // nd, cols), f32),
            pltpu.VMEM((nd, vrows, cols), bf16),
            dma((ROUNDS, 2, nt - 1)),
            dma((ROUNDS, 2, nt - 1)),
            dma((ROUNDS, 3, nd - 1)),
            dma((ROUNDS, 3, nd - 1)),
            dma((nd - 1,)),
            dma((nd - 1,)),
            dma((nd - 1,)),
            dma((nd - 1,)),
            dma((3 * mats + 3,)),
        ],
        compiler_params=pltpu.CompilerParams(
            collective_id=0, has_side_effects=True, vmem_limit_bytes=61 << 20
        ),
    )(grads_t, errors_t, jnp.swapaxes(start, 1, 2), moments, weights, vector_grads)
    new_errors, new_moments, new_weights, new_vmom, new_vwgt = pl.pallas_call(
        functools.partial(apply_kernel, nd, rank),
        out_shape=(
            jax.ShapeDtypeStruct(errors_t.shape, f32),
            jax.ShapeDtypeStruct(moments.shape, f32),
            jax.ShapeDtypeStruct((mats, cols, rows), bf16),
            jax.ShapeDtypeStruct(vector_moments.shape, f32),
            jax.ShapeDtypeStruct(vector_weights.shape, f32),
        ),
        in_specs=[vmem] * 9,
        out_specs=(vmem,) * 5,
        compiler_params=pltpu.CompilerParams(vmem_limit_bytes=32 << 20),
    )(
        grads_t,
        errors_t,
        basis,
        right,
        weights_t,
        vector_sum,
        moments,
        vector_moments,
        vector_weights,
    )
    return (
        jnp.swapaxes(new_errors, 2, 3),
        new_moments,
        jnp.swapaxes(new_weights, 1, 2),
        new_vmom,
        new_vwgt,
    )


def fits(nd, nt, mats, rows, rank):
    stack = mats * rank
    return (
        mats == 2
        and LANES == 4 * rank
        and nd % 2 == 0
        and nt > 1
        and stack % (8 * nt) == 0
        and stack % (8 * nd) == 0
        and rows % (8 * nd) == 0
    )


def dispatch(nd, nt, *args):
    gradients, start = args[0], args[2]
    if fits(nd, nt, gradients.shape[1], gradients.shape[2], start.shape[2]):
        return two_kernels(nd, nt, *args)
    return per_device(*args)


def solution(mesh):
    in_specs = (
        P("dp", None, None, "tensor"),
        P("dp", None, None, "tensor"),
        P(None, "tensor", None),
        P(None, "dp", "tensor"),
        P(None, "dp", "tensor"),
        P("dp", None, "tensor"),
        P(None, "tensor"),
        P(None, "tensor"),
    )
    out_specs = (
        P("dp", None, None, "tensor"),
        P(None, "dp", "tensor"),
        P(None, None, "tensor"),
        P(None, "tensor"),
        P(None, "tensor"),
    )
    return jax.shard_map(
        functools.partial(dispatch, mesh.shape["dp"], mesh.shape["tensor"]),
        mesh=mesh,
        in_specs=in_specs,
        out_specs=out_specs,
        check_vma=False,
    )
```
